128 devices in a mesh: row: 4 (over z), col: 16 (over x_hi, y, core), smp: 2 (over x_lo).
Axes of the slice: x: 4 (x_hi: 2, x_lo: 2; x = x_hi * 2 + x_lo), y: 4, z: 4, core: 2. Of those that a mesh axis runs over, the one named last changes fastest.
Arguments:
- pair_repr: bfloat16 [512, 512, 128], P('row', 'col'), may hold values from -6 to 6
- tri_weight: bfloat16 [128, 512], replicated, may hold values from -0.75 to 0.75
- tri_bias_weight: bfloat16 [128, 4], replicated, may hold values from -40 to 40
- tri_output_weight: bfloat16 [128, 128], replicated, may hold values from -0.5 to 0.5
- samples: bfloat16 [8, 512, 768], P('smp'), may hold values from -6 to 6
- levels: int32 [8], P('smp'), may hold values from 0 to 199
- single_cond: bfloat16 [512, 384], replicated, may hold values from -6 to 6
- noise_weight: bfloat16 [256, 384], replicated, may hold values from -0.375 to 0.375
- modulation_weight: bfloat16 [384, 1536], replicated, may hold values from -0.3125 to 0.3125
- attention_weight: bfloat16 [768, 3072], replicated, may hold values from -0.5 to 0.5
- pair_bias_weight: bfloat16 [128, 16], replicated, may hold values from -40 to 40
- output_weight: bfloat16 [768, 768], replicated, may hold values from -0.21875 to 0.21875
- output_gate_weight: bfloat16 [384, 768], replicated, may hold values from -0.3125 to 0.3125
Outputs:
- new_pair: bfloat16 [512, 512, 128], P('row', 'col')
- attn_update: bfloat16 [8, 512, 768], P('smp', ('row', 'col'))
The draws below stay inside these ranges and needn't reach their ends.
All inputs are finite; a program needn't handle non-finite values.
Results may differ from the reference program's by a relative error of at most 0.02.
The reference program's roundings to bfloat16 on the way count: a program that leaves them out, or rounds other values in their place, can miss the bound.
Values may be sent and summed in bfloat16 or wider, within the bound.
A program may use at most 128 MiB of HBM per device.

```python
import math
import jax
import jax.numpy as jnp
from jax import lax

CZ = 128
HT = 4
DT = 32
CA = 768
HD = 16
DH = 48
CS = 384
NE = 256
LEVELS = 200
N = 512
SAMPLES = 8


def bias_weights(key, channels, head_count):
    normal_part = jax.random.normal(jax.random.fold_in(key, 17), (channels, head_count), jnp.float32) * (2.5 / math.sqrt(channels))
    return jnp.clip(normal_part, -40.0, 40.0)


def draw_tri_bias_weight(key, part):
    return bias_weights(jax.random.fold_in(key, 3), CZ, HT).astype(jnp.bfloat16)


def draw_pair_bias_weight(key, part):
    return bias_weights(jax.random.fold_in(key, 5), CZ, HD).astype(jnp.bfloat16)


def draw_tri_weight(key, part):
    width = HT * DT
    spread = CZ ** (-0.5)
    base = jax.random.normal(jax.random.fold_in(key, 71), (CZ, 4 * width), jnp.float32) * spread
    base = jnp.clip(base, -6.0 * spread, 6.0 * spread)
    return jnp.clip(base, -0.75, 0.75).astype(jnp.bfloat16)


def draw_attention_weight(key, part):
    spread = CA ** (-0.5)
    base = jax.random.normal(jax.random.fold_in(key, 41), (CA, 4 * CA), jnp.float32) * spread
    base = jnp.clip(base, -6.0 * spread, 6.0 * spread)
    return jnp.clip(base, -0.5, 0.5).astype(jnp.bfloat16)


def with_ends(values, stream_key, smallest, high):
    longest = values.shape.index(max(values.shape))
    spots = []
    for shift in (0, 1):
        where = [jax.random.randint(jax.random.fold_in(stream_key, axis), (), 0, length) for axis, length in enumerate(values.shape)]
        where[longest] = (where[longest] + shift) % values.shape[longest]
        spots.append(tuple(where))
    return values.at[spots[0]].set(smallest).at[spots[1]].set(high)


def block_levels(stream_key, shape, shards, low, largest):
    gain, own = 1.0, jax.random.fold_in(stream_key, 6)
    for axis_at, parts in shards:
        heights = jnp.exp(jax.random.uniform(jax.random.fold_in(own, axis_at), (parts,), jnp.float32, low / len(shards), largest / len(shards)))
        gain = gain * jnp.repeat(heights, shape[axis_at] // parts).reshape([-1 if axis == axis_at else 1 for axis in range(len(shape))])
    return gain


def normal_values(key, dims, scale, limit, shards=(), kind=jnp.bfloat16):
    drawn = jax.random.normal(key, dims, jnp.float32) * scale
    if len(shards) > 0:
        drawn = block_levels(key, dims, shards, -0.22, 0.18) * drawn
    return jnp.clip(drawn, min=-limit, max=limit).astype(kind)


def setup_inputs(seed: int = 0) -> dict:
    keys = jax.random.split(jax.random.key(seed), 14)
    return {
        "pair_repr": normal_values(keys[0], (N, N, CZ), 1.0, 6.0, ((0, 4), (1, 16))),
        "tri_weight": draw_tri_weight(jax.random.fold_in(keys[13], 71), 0),
        "tri_bias_weight": draw_tri_bias_weight(jax.random.fold_in(keys[13], 71), 0),
        "tri_output_weight": normal_values(keys[3], (HT * DT, CZ), (HT * DT) ** -0.5, 0.5),
        "samples": normal_values(keys[4], (SAMPLES, N, CA), 1.0, 6.0, ((0, 2),)),
        "levels": with_ends(jax.random.randint(keys[5], (SAMPLES,), 0, LEVELS), jax.random.fold_in(keys[5], 1), 0, LEVELS - 1).astype(jnp.int32),
        "single_cond": normal_values(keys[6], (N, CS), 1.0, 6.0),
        "noise_weight": normal_values(keys[7], (NE, CS), NE ** -0.5, 0.375),
        "modulation_weight": normal_values(keys[8], (CS, 2 * CA), CS ** -0.5, 0.3125),
        "attention_weight": draw_attention_weight(jax.random.fold_in(keys[13], 71), 0),
        "pair_bias_weight": draw_pair_bias_weight(jax.random.fold_in(keys[13], 71), 0),
        "output_weight": normal_values(keys[11], (CA, CA), CA ** -0.5, 0.21875),
        "output_gate_weight": normal_values(keys[12], (CS, CA), CS ** -0.5, 0.3125),
    }


NORM_EPSILON = 1e-05
SIGMA_DATA = 16.0
SIGMA_MAX = 160.0
SIGMA_MIN = 0.0004

def normalize(values):
    values = values.astype(jnp.float32)
    average = lax.optimization_barrier(jnp.mean(values, axis=-1, keepdims=True))
    centred = values - average
    variance = lax.optimization_barrier(jnp.mean(centred * centred, axis=-1, keepdims=True))
    return centred * lax.rsqrt(variance + NORM_EPSILON)

def noise_features(levels):
    fraction = levels.astype(jnp.float32) / (LEVELS - 1)
    upper_root = SIGMA_MAX ** (1.0 / 7.0)
    lower_root = SIGMA_MIN ** (1.0 / 7.0)
    noise_sigma = SIGMA_DATA * (upper_root + fraction * (lower_root - upper_root)) ** 7
    scaled = 0.25 * jnp.log(noise_sigma / SIGMA_DATA)
    frequency = 2.0 * math.pi * jnp.exp(jnp.arange(NE // 2, dtype=jnp.float32) * (math.log(100.0) / (NE // 2)))
    angles = scaled[:, None] * frequency[None, :]
    return jnp.concatenate([jnp.cos(angles), jnp.sin(angles)], axis=-1)

def attend_columns(pair_cols, bias_full, tri_weight, tri_output_weight):
    row_count, col_count, channels = pair_cols.shape
    normed = normalize(pair_cols).astype(jnp.bfloat16)
    projected = jnp.dot(normed.reshape(row_count * col_count, channels), tri_weight, preferred_element_type=jnp.float32)
    projected = projected.reshape(row_count, col_count, 4, HT * DT)
    query_part = (projected[:, :, 0] * DT ** (-0.5)).astype(jnp.bfloat16)
    key_part = projected[:, :, 1].astype(jnp.bfloat16)
    value_part = projected[:, :, 2].astype(jnp.bfloat16)
    gate_part = projected[:, :, 3]

    def one_column(column):
        query_col = lax.dynamic_index_in_dim(query_part, column, 1, keepdims=False).reshape(row_count, HT, DT)
        key_col = lax.dynamic_index_in_dim(key_part, column, 1, keepdims=False).reshape(row_count, HT, DT)
        value_col = lax.dynamic_index_in_dim(value_part, column, 1, keepdims=False).reshape(row_count, HT, DT)
        gate_col = lax.dynamic_index_in_dim(gate_part, column, 1, keepdims=False)
        scores = jnp.einsum('ihd,khd->hik', query_col.astype(jnp.float32), key_col.astype(jnp.float32))
        scores = scores + bias_full
        row_peak = lax.optimization_barrier(jnp.max(scores, axis=-1, keepdims=True))
        exponent = jnp.exp(scores - row_peak)
        row_total = lax.optimization_barrier(jnp.sum(exponent, axis=-1))
        weights = exponent.astype(jnp.bfloat16)
        attended = jnp.einsum('hik,khd->ihd', weights.astype(jnp.float32), value_col.astype(jnp.float32))
        attended = attended / jnp.transpose(row_total)[:, :, None]
        return (jax.nn.sigmoid(gate_col) * attended.reshape(row_count, HT * DT)).astype(jnp.bfloat16)
    gated = lax.map(one_column, jnp.arange(col_count, dtype=jnp.int32))
    update = jnp.einsum('jic,cz->ijz', gated.astype(jnp.float32), tri_output_weight.astype(jnp.float32))
    return (pair_cols.astype(jnp.float32) + update).astype(jnp.bfloat16)

def reference(pair_repr, tri_weight, tri_bias_weight, tri_output_weight, samples, levels, single_cond, noise_weight, modulation_weight, attention_weight, pair_bias_weight, output_weight, output_gate_weight):
    normed = normalize(pair_repr).astype(jnp.bfloat16)
    bias_full = jnp.einsum('kiz,zh->hik', normed.astype(jnp.float32), tri_bias_weight.astype(jnp.float32))
    new_pair = attend_columns(pair_repr, bias_full, tri_weight, tri_output_weight)
    pair_renormed = normalize(new_pair).astype(jnp.bfloat16)
    pair_bias = jnp.einsum('ikz,zh->hik', pair_renormed.astype(jnp.float32), pair_bias_weight.astype(jnp.float32))
    features = noise_features(levels).astype(jnp.bfloat16)
    noise_terms = jnp.dot(features, noise_weight, preferred_element_type=jnp.float32)
    conditioned = normalize(single_cond.astype(jnp.float32)[None, :, :] + noise_terms[:, None, :]).astype(jnp.bfloat16)
    modulation = jnp.einsum('stc,cd->std', conditioned.astype(jnp.float32), modulation_weight.astype(jnp.float32))
    adapted = (jax.nn.sigmoid(modulation[..., :CA]) * normalize(samples) + modulation[..., CA:]).astype(jnp.bfloat16)
    out_gate = jax.nn.sigmoid(jnp.einsum('stc,cd->std', conditioned.astype(jnp.float32), output_gate_weight.astype(jnp.float32)))

    def one_sample(inputs):
        adapted_one, gate_one = inputs
        token_count = adapted_one.shape[0]
        projected = jnp.dot(adapted_one, attention_weight, preferred_element_type=jnp.float32)
        query_part = (projected[:, :CA] * DH ** (-0.5)).astype(jnp.bfloat16).reshape(token_count, HD, DH)
        key_part = projected[:, CA:2 * CA].astype(jnp.bfloat16).reshape(token_count, HD, DH)
        value_part = projected[:, 2 * CA:3 * CA].astype(jnp.bfloat16).reshape(token_count, HD, DH)
        gate_part = projected[:, 3 * CA:]
        scores = jnp.einsum('ihd,khd->hik', query_part.astype(jnp.float32), key_part.astype(jnp.float32)) + pair_bias
        row_peak = lax.optimization_barrier(jnp.max(scores, axis=-1, keepdims=True))
        exponent = jnp.exp(scores - row_peak)
        row_total = lax.optimization_barrier(jnp.sum(exponent, axis=-1))
        weights = exponent.astype(jnp.bfloat16)
        attended = jnp.einsum('hik,khd->ihd', weights.astype(jnp.float32), value_part.astype(jnp.float32))
        attended = attended / jnp.transpose(row_total)[:, :, None]
        gated = (jax.nn.sigmoid(gate_part) * attended.reshape(token_count, CA)).astype(jnp.bfloat16)
        projected_out = jnp.dot(gated, output_weight, preferred_element_type=jnp.float32)
        return (gate_one * projected_out).astype(jnp.bfloat16)
    attn_update = lax.map(one_sample, (adapted, out_gate))
    return (new_pair, attn_update)
```

```python
import math

import jax
import jax.numpy as jnp
from jax import lax
from jax.experimental import pallas as pl
from jax.experimental.pallas import tpu as pltpu
from jax.sharding import PartitionSpec as P

MESH = pl.DeviceIdType.MESH
F32 = jnp.float32
BF16 = jnp.bfloat16

DT = 32
CA = 768
HD = 16
DH = 48
NE = 256
LEVELS = 200

NORM_EPSILON = 1e-05
SIGMA_DATA = 16.0
SIGMA_MAX = 160.0
SIGMA_MIN = 0.0004

NT = (((1,), (1,)), ((), ()))


def normalize(values):
    values = values.astype(F32)
    average = jnp.mean(values, axis=-1, keepdims=True)
    centred = values - average
    variance = jnp.mean(centred * centred, axis=-1, keepdims=True)
    return centred * lax.rsqrt(variance + NORM_EPSILON)


def noise_features(levels):
    fraction = levels.astype(F32) / (LEVELS - 1)
    upper_root = SIGMA_MAX ** (1.0 / 7.0)
    lower_root = SIGMA_MIN ** (1.0 / 7.0)
    noise_sigma = SIGMA_DATA * (upper_root + fraction * (lower_root - upper_root)) ** 7
    scaled = 0.25 * jnp.log(noise_sigma / SIGMA_DATA)
    frequency = 2.0 * math.pi * jnp.exp(jnp.arange(NE // 2, dtype=F32) * (math.log(100.0) / (NE // 2)))
    angles = scaled[:, None] * frequency[None, :]
    return jnp.concatenate([jnp.cos(angles), jnp.sin(angles)], axis=-1)


def sigmoid(x):
    return 1.0 / (1.0 + jnp.exp(-x))


def dot(a, b):
    return jnp.dot(a, b, preferred_element_type=F32)


def dot_nt(a, b):
    return lax.dot_general(a, b, NT, preferred_element_type=F32)


def kernel(
    noise,
    wtri,
    tbw,
    wo_big,
    pbw_big,
    pair_h,
    samples_h,
    cond_h,
    modw_h,
    attw_h,
    ow_h,
    ogw_h,
    new_out,
    upd_out,
    pair_v,
    f32buf,
    norm_t,
    loc,
    cols,
    bias,
    qbuf,
    kvbuf,
    gatebuf,
    resbuf,
    gbuf,
    grecv,
    renorm,
    pb_t,
    pb_recv,
    samples_v,
    cond_v,
    samp_own,
    cond_own,
    modw,
    attw,
    ow,
    ogw,
    kv_all,
    q_own,
    gate_own,
    og_own,
    att_all,
    lsem,
    ssem,
    rsem,
    gssem,
    grsem,
):
    r = lax.axis_index("row")
    c = lax.axis_index("col")
    s = lax.axis_index("smp")
    xh = c // 8
    y = (c // 2) % 4
    core = c % 2
    so = 1 - s
    c8 = (c + 8) % 16
    token = pl.multiple_of(r * 128 + c * 8, 8)

    barrier = pltpu.get_barrier_semaphore()

    def col_peer(d):
        b = (c + d) % 16
        return (r, b, (s + b // 8 + xh) % 2)

    def row_peer(d, e):
        return ((r + d) % 4, c, (s + e) % 2)

    greet = [row_peer(d, e) for d in range(4) for e in range(2) if d + e > 0]
    greet += [col_peer(d) for d in range(1, 16)]
    for peer in greet:
        pl.semaphore_signal(barrier, inc=1, device_id=peer, device_id_type=MESH)

    loads = [
        pltpu.make_async_copy(src, dst, lsem.at[n])
        for n, (src, dst) in enumerate(
            [
                (pair_h, pair_v),
                (cond_h, cond_v),
                (modw_h, modw),
                (samples_h, samples_v),
                (attw_h, attw),
                (samples_h.at[:, pl.ds(token, 8), :], samp_own),
                (cond_h.at[pl.ds(token, 8), :], cond_own),
                (ogw_h, ogw),
                (ow_h, ow),
            ]
        )
    ]
    for load in loads:
        load.start()

    loads[0].wait()

    def norm_step(t, carry):
        x = pair_v[pl.ds(t * 8, 8)].astype(F32).reshape(256, 128)
        f32buf[pl.ds(pl.multiple_of(t * 256, 256), 256), :] = normalize(x)
        return carry

    lax.fori_loop(0, 16, norm_step, 0)

    def turn_step(i, carry):
        v = f32buf[pl.ds(i, 128, stride=32), :].astype(BF16)
        norm_t[i] = v
        out = dot_nt(tbw[...], v)
        for h in range(4):
            loc[h, pl.ds(i, 1), :] = out[h : h + 1]
        return carry

    lax.fori_loop(0, 32, turn_step, 0)
    bias[c, r] = loc[pl.ds(2 * s, 2)]
    cols[r] = norm_t[pl.ds(8 * r, 8)]

    pl.semaphore_wait(barrier, len(greet))

    def send(n, src, dst, dev):
        return pltpu.make_async_remote_copy(
            src_ref=src,
            dst_ref=dst,
            send_sem=ssem.at[n],
            recv_sem=rsem.at[n],
            device_id=dev,
            device_id_type=MESH,
        )

    zp = ((r + 1) % 4, c, s)
    zm = ((r + 3) % 4, c, s)
    rm, rp = (r + 3) % 4, (r + 1) % 4

    def ycol(d):
        return xh * 8 + ((y + d) % 4) * 2 + core

    cp, c2, cm = ycol(1), ycol(2), ycol(3)
    cp8, c28, cm8 = (cp + 8) % 16, (c2 + 8) % 16, (cm + 8) % 16
    yp, ym = (r, cp, s), (r, cm, s)
    peer_core = (r, c + 1 - 2 * core, s)

    copies = {}
    copies[3] = send(3, loc.at[pl.ds(2 * so, 2)], bias.at[c, r], (r, c8, so))
    copies[4] = send(4, bias.at[c, r], bias.at[c, r], zp)
    copies[5] = send(5, bias.at[c, r], bias.at[c, r], zm)
    copies[6] = send(6, bias.at[c, rm], bias.at[c, rm], zp)
    copies[7] = send(7, bias.at[c8, r], bias.at[c8, r], zp)
    copies[8] = send(8, bias.at[c8, r], bias.at[c8, r], zm)
    copies[9] = send(9, bias.at[c8, rp], bias.at[c8, rp], zm)
    for n, unit, dev in (
        (10, c, yp),
        (11, c, ym),
        (12, cm, yp),
        (13, c8, yp),
        (14, c8, ym),
        (15, cp8, ym),
        (16, c, peer_core),
        (17, c8, peer_core),
        (18, cm, peer_core),
        (19, cp, peer_core),
        (20, c2, peer_core),
        (21, cm8, peer_core),
        (22, cp8, peer_core),
        (23, c28, peer_core),
    ):
        copies[n] = send(n, bias.at[unit], bias.at[unit], dev)
    for d in (1, 2, 3):
        dest = (r + d) % 4
        copies[d - 1] = send(d - 1, norm_t.at[pl.ds(8 * dest, 8)], cols.at[r], (dest, c, s))

    def start(*which):
        for n in which:
            copies[n].start()

    def arrived(*which):
        for n in which:
            copies[n].wait_recv()

    def kv_step(ch, carry):
        s4 = ch // 2
        t = pl.multiple_of((ch % 2) * 256, 256)
        trunk = cond_v[pl.ds(t, 256), :].astype(F32) + noise[pl.ds(s4, 1), :]
        m = dot(normalize(trunk).astype(BF16), modw[...])
        act = normalize(samples_v[s4, pl.ds(t, 256), :])
        ad = (sigmoid(m[:, :CA]) * act + m[:, CA:]).astype(BF16)
        at = pl.multiple_of(ch * 256, 256)
        kv_all[pl.ds(at, 256), :] = dot(ad, attw[:, CA : 3 * CA]).astype(BF16)
        return carry

    def filler(lo, hi):
        lax.fori_loop(lo, hi, kv_step, 0)

    start(3, 4, 5, 0, 1, 2)
    for load in loads[1:]:
        load.wait()
    arrived(3)
    start(7, 8)
    filler(0, 1)
    arrived(4)
    start(6)
    arrived(8)
    start(9)
    filler(1, 2)
    arrived(5, 6, 7, 9)
    start(10, 11, 13, 14, 16, 17)
    filler(2, 4)
    arrived(10)
    start(12, 18)
    arrived(14)
    start(15, 22)
    arrived(11)
    start(19)
    arrived(13)
    start(21)
    filler(4, 8)
    arrived(12)
    start(20)
    arrived(15)
    start(23)

    trunk = cond_own[...].astype(F32)
    trunk = jnp.concatenate([trunk + noise[k : k + 1, :] for k in range(4)], axis=0)
    cond_n = normalize(trunk).astype(BF16)
    m = dot(cond_n, modw[...])
    act = normalize(samp_own[...].astype(F32).reshape(32, CA))
    ad = (sigmoid(m[:, :CA]) * act + m[:, CA:]).astype(BF16)
    q_own[...] = dot(ad, attw[:, :CA]) * DH ** (-0.5)
    gate_own[...] = sigmoid(dot(ad, attw[:, 3 * CA :]))
    og_own[...] = sigmoid(dot(cond_n, ogw[...]))

    arrived(0, 1, 2, *range(16, 24))

    lane = lax.broadcasted_iota(jnp.int32, (128, 128), 1)

    def back(jp, d, e):
        dest = (r + d) % 4
        n = d * 2 + e - 1
        return pltpu.make_async_remote_copy(
            src_ref=gbuf.at[jp, dest],
            dst_ref=grecv.at[s, r, jp],
            send_sem=gssem.at[jp, n],
            recv_sem=grsem.at[jp, n],
            device_id=(dest, c, (s + e) % 2),
            device_id_type=MESH,
        )

    returns = [(d, e) for d in range(4) for e in range(2) if d + e > 0]

    def pair_step(jp, carry):
        for jj in range(2):
            x = cols[:, jp * 2 + jj].reshape(512, 128)
            qg = dot(x, wtri[:, :128])
            qbuf[...] = (qg * DT ** (-0.5)).astype(BF16)
            gatebuf[...] = sigmoid(qg)
            kvbuf[...] = dot(x, wtri[:, 128:]).astype(BF16)

            def chunk_step(ic, carry):
                rows = pl.ds(pl.multiple_of(ic * 128, 128), 128)
                q = qbuf[rows, :]
                parts = []
                for h in range(2):
                    qm = jnp.where((lane >= 32 * h) & (lane < 32 * h + 32), q, jnp.zeros_like(q))
                    add = jnp.concatenate(
                        [bias[pl.ds(ic * 4, 4), k, h].reshape(128, 128) for k in range(4)], axis=1
                    )
                    sc = dot_nt(qm, kvbuf[...]) + add
                    e = jnp.exp(sc - jnp.max(sc, axis=-1, keepdims=True))
                    total = jnp.sum(e, axis=-1, keepdims=True)
                    parts.append(dot(e.astype(BF16), kvbuf[...]) / total)
                res = jnp.where(lane < 96, parts[0], parts[1]) * gatebuf[rows, :]
                if jj == 0:
                    resbuf[rows, :] = pltpu.roll(res, 64, 1)
                else:
                    gbuf[jp, ic] = jnp.where(lane < 64, resbuf[rows, :], res).astype(BF16)
                return carry

            lax.fori_loop(0, 4, chunk_step, 0)
        for d, e in returns:
            back(jp, d, e).start()
        grecv[s, r, jp] = gbuf[jp, r]
        return carry

    lax.fori_loop(0, 4, pair_step, 0)

    def wait_step(jp, carry):
        for d, e in returns:
            back(jp, d, e).wait_recv()
        return carry

    lax.fori_loop(0, 4, wait_step, 0)

    def project_step(n, carry):
        src = n // 4
        jp = n % 4
        lhs = jnp.concatenate([grecv[0, src, jp], grecv[1, src, jp]], axis=1)
        out = dot(lhs, wo_big[...])
        f32buf[pl.ds(2 * n, 128, stride=32), :] = out[:, :128]
        f32buf[pl.ds(2 * n + 1, 128, stride=32), :] = out[:, 128:]
        return carry

    lax.fori_loop(0, 16, project_step, 0)

    def new_step(t, carry):
        x = pair_v[pl.ds(t * 8, 8)].astype(F32).reshape(256, 128)
        new = (x + f32buf[pl.ds(pl.multiple_of(t * 256, 256), 256), :]).astype(BF16)
        new_out[pl.ds(t * 8, 8)] = new.reshape(8, 32, 128)
        renorm[pl.ds(t * 8, 8)] = normalize(new).astype(BF16).reshape(8, 32, 128)
        return carry

    lax.fori_loop(0, 16, new_step, 0)

    acc = None
    for half in range(4):
        lhs = jnp.concatenate(
            [renorm[pl.ds(2 * half + k, 16, stride=8)].reshape(512, 128) for k in range(2)], axis=1
        )
        part = dot(lhs, pbw_big[256 * half : 256 * half + 256, :])
        acc = part if acc is None else acc + part
    pb_t[...] = acc.reshape(16, 32, 128)

    for d in range(1, 16):
        b = (c + d) % 16
        copies[23 + d] = send(23 + d, pb_t.at[b], pb_recv.at[c], col_peer(d))
        copies[23 + d].start()
    pb_recv[c] = pb_t[c]
    arrived(*range(24, 39))

    row_id = lax.broadcasted_iota(jnp.int32, (128, CA), 0)
    lane_id = lax.broadcasted_iota(jnp.int32, (128, CA), 1)
    head0 = (row_id % 16) * DH
    mask = (lane_id >= head0) & (lane_id < head0 + DH)

    def sample_step(k, carry):
        q = q_own[pl.ds(pl.multiple_of(k * 8, 8), 8), :]
        qb = jnp.broadcast_to(q[:, None, :], (8, 16, CA)).reshape(128, CA)
        qb = jnp.where(mask, qb, 0.0).astype(BF16)
        at = pl.ds(pl.multiple_of(k * 512, 512), 512)
        sc = dot_nt(kv_all[at, :CA], qb) + pb_recv[...].reshape(512, 128)
        e = jnp.exp(sc - jnp.max(sc, axis=0, keepdims=True))
        et = e.T
        total = jnp.sum(et, axis=-1, keepdims=True)
        out = dot(et.astype(BF16), kv_all[at, CA:]) / total
        out = jnp.where(mask, out, 0.0).reshape(8, 16, CA)
        att_all[pl.ds(pl.multiple_of(k * 8, 8), 8), :] = jnp.sum(out, axis=1)
        return carry

    lax.fori_loop(0, 4, sample_step, 0)
    gated = (gate_own[...] * att_all[...]).astype(BF16)
    upd_out[...] = (og_own[...] * dot(gated, ow[...])).astype(BF16).reshape(4, 8, CA)

    for n in range(39):
        copies[n].wait_send()

    def drain_step(jp, carry):
        for d, e in returns:
            back(jp, d, e).wait_send()
        return carry

    lax.fori_loop(0, 4, drain_step, 0)


def local(
    pair_repr,
    tri_weight,
    tri_bias_weight,
    tri_output_weight,
    samples,
    levels,
    single_cond,
    noise_weight,
    modulation_weight,
    attention_weight,
    pair_bias_weight,
    output_weight,
    output_gate_weight,
):
    s = lax.axis_index("smp")
    noise = jnp.dot(noise_features(levels).astype(BF16), noise_weight, preferred_element_type=F32)
    halves = lax.dynamic_slice_in_dim(tri_weight.reshape(128, 4, 2, 64), s, 1, 2)[:, :, 0]
    wtri = jnp.concatenate([halves[:, 0], halves[:, 3], halves[:, 1], halves[:, 2]], axis=1)
    tbw = jnp.pad(tri_bias_weight.T, ((0, 12), (0, 0)))
    zero = jnp.zeros((64, 128), BF16)
    wo_big = jnp.concatenate(
        [
            jnp.concatenate([tri_output_weight[64 * p : 64 * p + 64] if k == jj else zero for k in range(2)], axis=1)
            for p in range(2)
            for jj in range(2)
        ],
        axis=0,
    )
    eye = jnp.eye(8, dtype=BF16)
    pbw_big = (eye[:, None, :, None] * pair_bias_weight[None, :, None, :]).reshape(1024, 128)
    vm = pl.BlockSpec(memory_space=pltpu.VMEM)
    hbm = pl.BlockSpec(memory_space=pl.ANY)
    dma = pltpu.SemaphoreType.DMA
    return pl.pallas_call(
        kernel,
        out_shape=(
            jax.ShapeDtypeStruct((128, 32, 128), BF16),
            jax.ShapeDtypeStruct((4, 8, CA), BF16),
        ),
        in_specs=[vm] * 5 + [hbm] * 7,
        out_specs=(vm, vm),
        scratch_shapes=[
            pltpu.VMEM((128, 32, 128), BF16),
            pltpu.VMEM((4096, 128), F32),
            pltpu.VMEM((32, 128, 128), BF16),
            pltpu.VMEM((4, 32, 128), F32),
            pltpu.VMEM((4, 8, 128, 128), BF16),
            pltpu.VMEM((16, 4, 2, 32, 128), F32),
            pltpu.VMEM((512, 128), BF16),
            pltpu.VMEM((512, 128), BF16),
            pltpu.VMEM((512, 128), F32),
            pltpu.VMEM((512, 128), F32),
            pltpu.VMEM((4, 4, 128, 128), BF16),
            pltpu.VMEM((2, 4, 4, 128, 128), BF16),
            pltpu.VMEM((128, 32, 128), BF16),
            pltpu.VMEM((16, 32, 128), F32),
            pltpu.VMEM((16, 32, 128), F32),
            pltpu.VMEM((4, 512, CA), BF16),
            pltpu.VMEM((512, 384), BF16),
            pltpu.VMEM((4, 8, CA), BF16),
            pltpu.VMEM((8, 384), BF16),
            pltpu.VMEM((384, 2 * CA), BF16),
            pltpu.VMEM((CA, 4 * CA), BF16),
            pltpu.VMEM((CA, CA), BF16),
            pltpu.VMEM((384, CA), BF16),
            pltpu.VMEM((2048, 2 * CA), BF16),
            pltpu.VMEM((32, CA), F32),
            pltpu.VMEM((32, CA), F32),
            pltpu.VMEM((32, CA), F32),
            pltpu.VMEM((32, CA), F32),
            dma((9,)),
            dma((39,)),
            dma((39,)),
            dma((4, 7)),
            dma((4, 7)),
        ],
        compiler_params=pltpu.CompilerParams(
            collective_id=0, has_side_effects=True, vmem_limit_bytes=62 * 1024 * 1024
        ),
        name="pair_and_samples",
    )(
        noise,
        wtri,
        tbw,
        wo_big,
        pbw_big,
        pair_repr,
        samples,
        single_cond,
        modulation_weight,
        attention_weight,
        output_weight,
        output_gate_weight,
    )


def solution(mesh):
    return jax.shard_map(
        local,
        mesh=mesh,
        in_specs=(
            P("row", "col", None),
            P(),
            P(),
            P(),
            P("smp", None, None),
            P("smp"),
            P(),
            P(),
            P(),
            P(),
            P(),
            P(),
            P(),
        ),
        out_specs=(P("row", "col", None), P("smp", ("row", "col"), None)),
        check_vma=False,
    )
```
